32 devices in a mesh: groups: 2 (over x), seq: 16 (over z, y, core).
Axes of the slice: x: 2, y: 2, z: 4, core: 2. Of those that a mesh axis runs over, the one named last changes fastest.
Arguments:
- tokens: bfloat16 [96, 5120], P(('groups', 'seq')), parts along dimension 0, may hold values from -6 to 6
- modulation: float32 [6, 5120], replicated, may hold values from -2.5 to 2.5
- w_qkv: bfloat16 [3, 5120, 2560], P(None, None, 'seq'), may hold values from -0.078125 to 0.078125
- norm_gains: float32 [2, 2560], replicated, may hold values from 0.56 to 12
- cache_kv: bfloat16 [2, 2, 96, 2560], P(None, None, ('groups', 'seq')), parts along dimension 2, may hold values from -17 to 17
- w_out: bfloat16 [2560, 5120], P(None, 'seq'), may hold values from -0.125 to 0.125
- w_up: bfloat16 [5120, 13824], P(None, 'seq'), may hold values from -0.078125 to 0.078125
- w_down: bfloat16 [13824, 5120], P('seq'), may hold values from -0.0546875 to 0.0546875
Outputs:
- block_out: bfloat16 [96, 5120], P(('groups', 'seq')), parts along dimension 0
The draws below stay inside these ranges and needn't reach their ends.
There are 2 independent parts, one for each index of `groups`. The reference program is written for one: setup_inputs(seed, part) draws one part's arguments, and reference() takes and returns one part's arrays. A program takes and returns all parts, laid end to end along the dimension named above; an argument that names none is the same for every part. Nothing has to cross between parts.
All inputs are finite; a program needn't handle non-finite values.
Results may differ from the reference program's by a relative error of at most 0.017.
The reference program's roundings to bfloat16 on the way (of `normed`, `qkv`, `weights`, `attended`, `projected`, `normed2` and `hidden`) count: a program that leaves them out, or rounds other values in their place, can miss the bound.
Values may be sent and summed in bfloat16 or wider, within the bound.
A program may use at most 128 MiB of HBM per device.

```python
import math
import jax
import jax.numpy as jnp
from jax import lax

D = 5120
FF = 13824
HEAD_DIM = 128
HEADS = 20
FRAMES = 2
ATTN = 2560
TOKENS = 48


def draw_norm_gains(key, part):
    key_one, key_two = jax.random.split(jax.random.fold_in(key, 11))
    lower, upper = (0.7, 1.6)
    head_scale = jnp.exp(jax.random.uniform(key_one, (2, HEADS, 1), jnp.float32, math.log(lower), math.log(upper)))
    channel = jax.random.uniform(key_two, (2, HEADS, HEAD_DIM), jnp.float32, 0.8, 1.2)
    return (head_scale * channel).reshape(2, HEADS * HEAD_DIM)


def draw_cache_kv(key, part):
    key_one, key_two, key_three = jax.random.split(jax.random.fold_in(key, 23), 3)
    shape = (FRAMES, TOKENS, HEADS, HEAD_DIM)
    head_scale = jnp.exp(jax.random.uniform(key_one, (1, 1, HEADS, 1), jnp.float32, math.log(0.7), math.log(1.6)))
    keys = jnp.clip(jax.random.normal(key_two, shape, jnp.float32), -4.0, 4.0) * head_scale
    values = jnp.clip(jax.random.normal(key_three, shape, jnp.float32), -4.0, 4.0)
    stacked = jnp.stack([keys, values]).reshape(2, FRAMES, TOKENS, HEADS * HEAD_DIM)
    return stacked.astype(jnp.bfloat16)


def levels(rng, dims, cuts, least, top_value):
    loudness, own = 1.0, jax.random.fold_in(rng, 6)
    for position, parts in cuts:
        heights = jnp.exp(jax.random.uniform(jax.random.fold_in(own, position), (parts,), jnp.float32, least / len(cuts), top_value / len(cuts)))
        loudness = loudness * jnp.repeat(heights, dims[position] // parts).reshape([-1 if axis == position else 1 for axis in range(len(dims))])
    return loudness


def scatter_about(own_key, shape, scale, reach, shards=(), dtype=jnp.bfloat16):
    values = scale * jax.random.normal(own_key, shape, jnp.float32)
    if shards:
        values = values * levels(own_key, shape, shards, -0.22, 0.18)
    return jnp.clip(values, -reach, reach).astype(dtype)


def setup_inputs(seed: int = 0, part: int = 0) -> dict:
    key_of = jax.random.split(jax.random.key(seed), 9)
    part_splits = jax.random.split(jax.random.fold_in(key_of[8], part), 9)
    return {
        "tokens": scatter_about(part_splits[0], (TOKENS, D), 1.0, 6.0, ((0, 16),)),
        "modulation": scatter_about(key_of[1], (6, D), 0.6, 2.5, (), jnp.float32),
        "w_qkv": scatter_about(key_of[2], (3, D, ATTN), D ** -0.5, 0.078125, ((2, 16),)),
        "norm_gains": draw_norm_gains(jax.random.fold_in(key_of[8], 71), part),
        "cache_kv": draw_cache_kv(jax.random.fold_in(jax.random.fold_in(key_of[8], part), 71), part),
        "w_out": scatter_about(key_of[5], (ATTN, D), ATTN ** -0.5, 0.125, ((1, 16),)),
        "w_up": scatter_about(key_of[6], (D, FF), D ** -0.5, 0.078125, ((1, 16),)),
        "w_down": scatter_about(key_of[7], (FF, D), FF ** -0.5, 0.0546875, ((0, 16),)),
    }


def layer_norm(values):
    center = values - lax.optimization_barrier(jnp.mean(values, axis=-1, keepdims=True))
    spread = lax.optimization_barrier(jnp.mean(center * center, axis=-1, keepdims=True))
    return center * lax.rsqrt(spread + 1e-06)

def rms_norm(values, gain):
    return values * lax.rsqrt(lax.optimization_barrier(jnp.mean(values * values, axis=-1, keepdims=True)) + 1e-06) * gain

def reference(tokens, modulation, w_qkv, norm_gains, cache_kv, w_out, w_up, w_down):
    residual = tokens.astype(jnp.float32)
    normed = (layer_norm(residual) * (1.0 + modulation[1]) + modulation[0]).astype(jnp.bfloat16)
    qkv = [jnp.dot(normed, w_qkv[index], preferred_element_type=jnp.float32).astype(jnp.bfloat16) for index in range(3)]
    queries = rms_norm(qkv[0].astype(jnp.float32), norm_gains[0]).astype(jnp.bfloat16)
    keys_now = rms_norm(qkv[1].astype(jnp.float32), norm_gains[1]).astype(jnp.bfloat16)
    keys = jnp.concatenate([cache_kv[0].reshape(FRAMES * TOKENS, ATTN), keys_now], axis=0)
    values = jnp.concatenate([cache_kv[1].reshape(FRAMES * TOKENS, ATTN), qkv[2]], axis=0)
    scale = 1.0 / math.sqrt(HEAD_DIM)
    query_heads = queries.reshape(TOKENS, HEADS, HEAD_DIM).transpose(1, 0, 2)
    key_heads = keys.reshape(-1, HEADS, HEAD_DIM).transpose(1, 0, 2)
    value_heads = values.reshape(-1, HEADS, HEAD_DIM).transpose(1, 0, 2)

    def one_head(operands):
        query_h, key_h, value_h = operands
        scores = jnp.dot(query_h, key_h.T, preferred_element_type=jnp.float32) * scale
        peak = lax.optimization_barrier(jnp.max(scores, axis=-1, keepdims=True))
        expo = jnp.exp(scores - peak)
        total = lax.optimization_barrier(jnp.sum(expo, axis=-1, keepdims=True))
        weights = expo.astype(jnp.bfloat16)
        return jnp.dot(weights, value_h, preferred_element_type=jnp.float32) / total
    heads_out = lax.map(one_head, (query_heads, key_heads, value_heads))
    attended = heads_out.transpose(1, 0, 2).reshape(TOKENS, ATTN).astype(jnp.bfloat16)
    projected = jnp.dot(attended, w_out, preferred_element_type=jnp.float32).astype(jnp.bfloat16)
    residual = residual + modulation[2] * projected.astype(jnp.float32)
    normed2 = (layer_norm(residual) * (1.0 + modulation[4]) + modulation[3]).astype(jnp.bfloat16)
    hidden = jax.nn.gelu(jnp.dot(normed2, w_up, preferred_element_type=jnp.float32), approximate=True).astype(jnp.bfloat16)
    feed = jnp.dot(hidden, w_down, preferred_element_type=jnp.float32)
    return (residual + modulation[5] * feed).astype(jnp.bfloat16)
```

```python
import math

import jax
import jax.numpy as jnp
from jax import lax
from jax.experimental import pallas as pl
from jax.experimental.pallas import tpu as pltpu
from jax.sharding import PartitionSpec as P

HEAD_DIM = 128
HEADS = 20
MESH = pl.DeviceIdType.MESH


def layer_norm(values):
    center = values - jnp.mean(values, axis=-1, keepdims=True)
    spread = jnp.mean(center * center, axis=-1, keepdims=True)
    return center * lax.rsqrt(spread + 1e-06)


def exchange(cid, n, gs, items):
    kinds = [kind for kind, _ in items]
    arrays = [array for _, array in items]
    count = len(items)
    outs = []
    for kind, array in items:
        block = array.shape if kind in ("all", "peer") else array.shape[1:]
        outs.append(jax.ShapeDtypeStruct(((gs if kind == "peer" else n),) + block, array.dtype))

    def body(*refs):
        ins, dsts = refs[:count], refs[count : 2 * count]
        send, recv, own = refs[2 * count :]
        me = lax.axis_index("seq")
        base = me - me % gs

        def source(k, j):
            if kinds[k] == "each":
                return ins[k].at[j]
            if kinds[k] == "block":
                return ins[k].at[j // gs]
            return ins[k]

        def other(k, i):
            if kinds[k] == "peer":
                return base + (me + i) % gs
            return (me + i) % n

        def row(k, j):
            return j % gs if kinds[k] == "peer" else j

        def steps(k):
            return gs if kinds[k] == "peer" else n

        barrier = pltpu.get_barrier_semaphore()

        def greet(i, c):
            pl.semaphore_signal(barrier, inc=1, device_id={"seq": (me + i) % n}, device_id_type=MESH)
            return c

        lax.fori_loop(1, n, greet, 0)
        locals_ = []
        for k in range(count):
            copy = pltpu.make_async_copy(source(k, me), dsts[k].at[row(k, me)], own.at[k])
            copy.start()
            locals_.append(copy)
        pl.semaphore_wait(barrier, n - 1)

        def remote(k, j, mark):
            return pltpu.make_async_remote_copy(
                src_ref=source(k, j),
                dst_ref=dsts[k].at[row(k, mark)],
                send_sem=send.at[k, j],
                recv_sem=recv.at[k, mark],
                device_id={"seq": j},
                device_id_type=MESH,
            )

        for k in range(count):
            def launch(i, c, k=k):
                remote(k, other(k, i), me).start()
                return c

            lax.fori_loop(1, steps(k), launch, 0)
        for copy in locals_:
            copy.wait()
        for k in range(count):
            def finish(i, c, k=k):
                j = other(k, i)
                copy = remote(k, j, j)
                copy.wait_recv()
                copy.wait_send()
                return c

            lax.fori_loop(1, steps(k), finish, 0)

    return pl.pallas_call(
        body,
        out_shape=outs,
        in_specs=[pl.BlockSpec(memory_space=pl.ANY)] * count,
        out_specs=[pl.BlockSpec(memory_space=pl.ANY)] * count,
        scratch_shapes=[
            pltpu.SemaphoreType.DMA((count, n)),
            pltpu.SemaphoreType.DMA((count, n)),
            pltpu.SemaphoreType.DMA((count,)),
        ],
        compiler_params=pltpu.CompilerParams(collective_id=cid, has_side_effects=True),
    )(*arrays)


def local(n, tokens, modulation, w_qkv, norm_gains, cache_kv, w_out, w_up, w_down):
    own_rows, features = tokens.shape
    width = HEADS * HEAD_DIM
    cols = w_qkv.shape[2]
    wide = math.lcm(cols, HEAD_DIM)
    gs = wide // cols
    blocks = n // gs
    heads = wide // HEAD_DIM
    frames = cache_kv.shape[1]
    total_rows = n * own_rows
    query_rows = total_rows // gs
    scale = 1.0 / math.sqrt(HEAD_DIM)
    me = lax.axis_index("seq")
    block, place = me // gs, me % gs

    (all_tokens,) = exchange(0, n, gs, [("all", tokens)])
    all_tokens = all_tokens.reshape(total_rows, features).astype(jnp.float32)
    normed = (layer_norm(all_tokens) * (1.0 + modulation[1]) + modulation[0]).astype(jnp.bfloat16)
    qkv_cols = [
        jnp.dot(normed, w_qkv[i], preferred_element_type=jnp.float32).astype(jnp.bfloat16) for i in range(3)
    ]
    squares = jnp.stack([jnp.sum(jnp.square(qkv_cols[i].astype(jnp.float32)), axis=-1) for i in range(2)])
    cache_blocks = cache_kv.reshape(2 * frames * own_rows, blocks, wide).transpose(1, 0, 2)
    cached, pieces, squares = exchange(
        1, n, gs, [("block", cache_blocks), ("peer", jnp.stack(qkv_cols)), ("all", squares)]
    )
    inverse = lax.rsqrt(jnp.sum(squares, axis=0) / width + 1e-06)
    pieces = pieces.transpose(1, 2, 0, 3).reshape(3, total_rows, wide)
    gains = lax.dynamic_slice_in_dim(norm_gains, block * wide, wide, axis=1)
    first = place * query_rows
    queries = (
        lax.dynamic_slice_in_dim(pieces[0], first, query_rows, axis=0).astype(jnp.float32)
        * lax.dynamic_slice_in_dim(inverse[0], first, query_rows, axis=0)[:, None]
        * gains[0]
    ).astype(jnp.bfloat16)
    keys_now = (pieces[1].astype(jnp.float32) * inverse[1][:, None] * gains[1]).astype(jnp.bfloat16)
    cached = cached.reshape(n, 2, frames * own_rows, wide).transpose(1, 0, 2, 3).reshape(2, -1, wide)
    keys = jnp.concatenate([cached[0], keys_now], axis=0).reshape(-1, heads, HEAD_DIM)
    values = jnp.concatenate([cached[1], pieces[2]], axis=0).reshape(-1, heads, HEAD_DIM)
    queries = queries.reshape(query_rows, heads, HEAD_DIM)
    scores = jnp.einsum("qhd,khd->hqk", queries, keys, preferred_element_type=jnp.float32) * scale
    expo = jnp.exp(scores - jnp.max(scores, axis=-1, keepdims=True))
    total = jnp.sum(expo, axis=-1, keepdims=True)
    summed = jnp.einsum("hqk,khd->hqd", expo.astype(jnp.bfloat16), values, preferred_element_type=jnp.float32)
    attended = (summed / total).astype(jnp.bfloat16).transpose(1, 0, 2).reshape(query_rows, wide)

    (attended,) = exchange(2, n, gs, [("all", attended)])
    attended = attended.reshape(blocks, total_rows, wide).transpose(1, 0, 2).reshape(total_rows, width)
    projected_cols = jnp.dot(attended, w_out, preferred_element_type=jnp.float32).astype(jnp.bfloat16)
    (projected,) = exchange(3, n, gs, [("all", projected_cols)])
    projected = projected.transpose(1, 0, 2).reshape(total_rows, features)
    residual = all_tokens + modulation[2] * projected.astype(jnp.float32)
    normed2 = (layer_norm(residual) * (1.0 + modulation[4]) + modulation[3]).astype(jnp.bfloat16)
    hidden = jax.nn.gelu(
        jnp.dot(normed2, w_up, preferred_element_type=jnp.float32), approximate=True
    ).astype(jnp.bfloat16)
    partial = jnp.dot(hidden, w_down, preferred_element_type=jnp.float32).astype(jnp.bfloat16)
    (partial,) = exchange(4, n, gs, [("each", partial.reshape(n, own_rows, features))])
    feed = jnp.sum(partial.astype(jnp.float32), axis=0)
    own = lax.dynamic_slice_in_dim(residual, me * own_rows, own_rows, axis=0)
    return (own + modulation[5] * feed).astype(jnp.bfloat16)


def solution(mesh):
    n = mesh.shape["seq"]
    in_specs = (
        P(("groups", "seq"), None),
        P(),
        P(None, None, "seq"),
        P(),
        P(None, None, ("groups", "seq"), None),
        P(None, "seq"),
        P(None, "seq"),
        P("seq", None),
    )
    out_specs = P(("groups", "seq"), None)

    def step(*args):
        return local(n, *args)

    return jax.shard_map(step, mesh=mesh, in_specs=in_specs, out_specs=out_specs, check_vma=False)
```

```python
import math

import jax
import jax.numpy as jnp
from jax import lax
from jax.experimental import pallas as pl
from jax.experimental.pallas import tpu as pltpu
from jax.sharding import PartitionSpec as P

HEAD_DIM = 128
HEADS = 20
MESH = pl.DeviceIdType.MESH


def layer_norm(values):
    center = values - jnp.mean(values, axis=-1, keepdims=True)
    spread = jnp.mean(center * center, axis=-1, keepdims=True)
    return center * lax.rsqrt(spread + 1e-06)


def factors(n):
    chips = n // 2
    near = 1
    while (2 * near) * (2 * near) <= chips:
        near *= 2
    return chips // near, near


def remote_copy(src, dst, send, recv, device):
    return pltpu.make_async_remote_copy(
        src_ref=src, dst_ref=dst, send_sem=send, recv_sem=recv, device_id={"seq": device}, device_id_type=MESH
    )


def loop(low, high, fn):
    def step(i, c):
        fn(i)
        return c

    lax.fori_loop(low, high, step, 0)


def greet(n, me):
    barrier = pltpu.get_barrier_semaphore()

    def signal(i):
        pl.semaphore_signal(barrier, inc=1, device_id={"seq": (me + i) % n}, device_id_type=MESH)

    loop(1, n, signal)
    return barrier


def exchange(cid, n, gs, items):
    kinds = [kind for kind, _ in items]
    arrays = [array for _, array in items]
    count = len(items)
    far, near = factors(n)
    outs = []
    for kind, array in items:
        block = array.shape[1:] if kind == "block" else array.shape
        outs.append(jax.ShapeDtypeStruct(((gs if kind == "peer" else n),) + block, array.dtype))

    def body(*refs):
        ins, dsts = refs[:count], refs[count : 2 * count]
        send, recv, own = refs[2 * count :]
        me = lax.axis_index("seq")
        base = me - me % gs
        a, b, c = me // (2 * near), (me // 2) % near, me % 2
        barrier = greet(n, me)

        def dev(a2, b2, c2):
            return (a2 * near + b2) * 2 + c2

        def first(k, a2):
            return ins[k].at[(a2 * 2 * near) // gs] if kinds[k] == "block" else ins[k]

        def far_copy(k, i, mark):
            a2 = (a + i) % far
            return remote_copy(first(k, a2), dsts[k].at[mark], send.at[k, 0, i], recv.at[k, mark], dev(a2, b, c))

        def near_copy(k, i, j):
            row = dev((a + far - i) % far, b, c)
            src = first(k, a) if isinstance(i, int) else dsts[k].at[row]
            return remote_copy(
                src, dsts[k].at[row], send.at[k, 1, i * near + j], recv.at[k, row], dev(a, (b + j) % near, c)
            )

        def core_copy(k, i, j):
            row = dev((a + far - i) % far, (b + near - j) % near, c)
            src = first(k, a) if isinstance(i, int) else dsts[k].at[row]
            return remote_copy(src, dsts[k].at[row], send.at[k, 2, i * near + j], recv.at[k, row], dev(a, b, 1 - c))

        def arrived(k, row):
            remote_copy(dsts[k].at[row], dsts[k].at[row], send.at[k, 0, 0], recv.at[k, row], me).wait_recv()

        def peer_copy(k, i, mark):
            return remote_copy(
                ins[k], dsts[k].at[mark], send.at[k, 0, i], recv.at[k, mark], base + (me + i) % gs
            )

        tree = [k for k in range(count) if kinds[k] != "peer"]
        direct = [k for k in range(count) if kinds[k] == "peer"]
        locals_ = []
        for k in range(count):
            if k in tree:
                copy = pltpu.make_async_copy(first(k, a), dsts[k].at[me], own.at[k])
            else:
                copy = pltpu.make_async_copy(ins[k], dsts[k].at[me % gs], own.at[k])
            copy.start()
            locals_.append(copy)
        pl.semaphore_wait(barrier, n - 1)
        for k in tree:
            loop(1, far, lambda i: far_copy(k, i, me).start())
        for k in direct:
            loop(1, gs, lambda i: peer_copy(k, i, me % gs).start())
        for k in tree:
            loop(1, near, lambda j: near_copy(k, 0, j).start())
            core_copy(k, 0, 0).start()
        for k in tree:

            def forward(i):
                arrived(k, dev((a + far - i) % far, b, c))
                loop(1, near, lambda j: near_copy(k, i, j).start())
                core_copy(k, i, 0 * i).start()

            loop(1, far, forward)
        for k in tree:

            def across(m):
                j, i = 1 + m // far, m % far
                arrived(k, dev((a + far - i) % far, (b + near - j) % near, c))
                core_copy(k, i, j).start()

            loop(0, far * (near - 1), across)
        for copy in locals_:
            copy.wait()
        for k in direct:

            def finish(i):
                peer_copy(k, i, (me + i) % gs).wait_recv()
                peer_copy(k, i, me % gs).wait_send()

            loop(1, gs, finish)
        for k in tree:
            loop(0, n // 2, lambda m: arrived(k, 2 * m + 1 - c))
            loop(1, far, lambda i: far_copy(k, i, me).wait_send())

            def drain(m):
                i, j = m // near, m % near
                core_copy(k, i, j).wait_send()

            loop(0, far * near, drain)
            loop(0, far * (near - 1), lambda m: near_copy(k, m % far, 1 + m // far).wait_send())

    return pl.pallas_call(
        body,
        out_shape=outs,
        in_specs=[pl.BlockSpec(memory_space=pl.ANY)] * count,
        out_specs=[pl.BlockSpec(memory_space=pl.ANY)] * count,
        scratch_shapes=[
            pltpu.SemaphoreType.DMA((count, 3, max(far * near, gs))),
            pltpu.SemaphoreType.DMA((count, n)),
            pltpu.SemaphoreType.DMA((count,)),
        ],
        compiler_params=pltpu.CompilerParams(collective_id=cid, has_side_effects=True),
    )(*arrays)


def reduce_exchange(cid, n, parts):
    far, near = factors(n)
    _, rows, features = parts.shape
    block = (rows, features)

    def body(x, out, got1, sum1, got2, sum2, got3, send, recv1, recv2, recv3):
        me = lax.axis_index("seq")
        a, b, c = me // (2 * near), (me // 2) % near, me % 2
        barrier = greet(n, me)

        def dev(a2, b2, c2):
            return (a2 * near + b2) * 2 + c2

        def spot(m):
            j, i = m // far, m % far
            return (a + 1 + i) % far, (b + 1 + j) % near

        def copy1(m):
            a2, b2 = spot(m)
            at = a2 * near + b2
            return remote_copy(x.at[dev(a2, b2, 1 - c)], got1.at[at], send.at[0, at], recv1.at[at], dev(a, b, 1 - c))

        def copy2(m, mark):
            a2, b2 = spot(m)
            at = a2 * near + b2
            return remote_copy(
                sum1.at[at], got2.at[a2 * near + mark], send.at[1, at], recv2.at[a2 * near + mark], dev(a, b2, c)
            )

        def copy3(i, mark):
            a2 = (a + i) % far
            return remote_copy(sum2.at[a2], got3.at[mark], send.at[2, a2], recv3.at[mark], dev(a2, b, c))

        def wide(v):
            return v.astype(jnp.float32)

        pl.semaphore_wait(barrier, n - 1)
        loop(0, far * near, lambda m: copy1(m).start())

        def pair(m):
            a2, b2 = spot(m)
            at = a2 * near + b2
            remote_copy(got1.at[at], got1.at[at], send.at[0, at], recv1.at[at], dev(a, b, 1 - c)).wait_recv()
            return wide(x[dev(a2, b2, c)]) + wide(got1[at])

        def hand(m):
            a2, b2 = spot(m)
            sum1[a2 * near + b2] = pair(m).astype(sum1.dtype)
            copy2(m, b).start()

        loop(0, far * (near - 1), hand)

        def collect(i):
            a2 = (a + i) % far
            total = pair(far * (near - 1) + i - 1)
            for j in range(1, near):
                at = a2 * near + (b + j) % near
                remote_copy(got2.at[at], got2.at[at], send.at[1, at], recv2.at[at], dev(a, b, 1 - c)).wait_recv()
                total = total + wide(got2[at])
            return a2, total

        def ship(i):
            a2, total = collect(i)
            sum2[a2] = total.astype(sum2.dtype)
            copy3(i, a).start()

        loop(1, far, ship)
        _, total = collect(far)
        for i in range(1, far):
            copy3(i, (a + i) % far).wait_recv()
            total = total + wide(got3[(a + i) % far])
        out[...] = total
        loop(0, far * near, lambda m: copy1(m).wait_send())
        loop(0, far * (near - 1), lambda m: copy2(m, b).wait_send())
        loop(1, far, lambda i: copy3(i, a).wait_send())

    dtype = parts.dtype
    return pl.pallas_call(
        body,
        out_shape=jax.ShapeDtypeStruct(block, jnp.float32),
        in_specs=[pl.BlockSpec(memory_space=pltpu.VMEM)],
        out_specs=pl.BlockSpec(memory_space=pltpu.VMEM),
        scratch_shapes=[
            pltpu.VMEM((far * near,) + block, dtype),
            pltpu.VMEM((far * near,) + block, dtype),
            pltpu.VMEM((far * near,) + block, dtype),
            pltpu.VMEM((far,) + block, dtype),
            pltpu.VMEM((far,) + block, dtype),
            pltpu.SemaphoreType.DMA((3, far * near)),
            pltpu.SemaphoreType.DMA((far * near,)),
            pltpu.SemaphoreType.DMA((far * near,)),
            pltpu.SemaphoreType.DMA((far,)),
        ],
        compiler_params=pltpu.CompilerParams(collective_id=cid, has_side_effects=True),
    )(parts)


def local(n, tokens, modulation, w_qkv, norm_gains, cache_kv, w_out, w_up, w_down):
    own_rows, features = tokens.shape
    width = HEADS * HEAD_DIM
    cols = w_qkv.shape[2]
    wide = math.lcm(cols, HEAD_DIM)
    gs = wide // cols
    blocks = n // gs
    heads = wide // HEAD_DIM
    frames = cache_kv.shape[1]
    total_rows = n * own_rows
    query_rows = total_rows // gs
    scale = 1.0 / math.sqrt(HEAD_DIM)
    me = lax.axis_index("seq")
    block, place = me // gs, me % gs

    (all_tokens,) = exchange(0, n, gs, [("all", tokens)])
    all_tokens = all_tokens.reshape(total_rows, features).astype(jnp.float32)
    normed = (layer_norm(all_tokens) * (1.0 + modulation[1]) + modulation[0]).astype(jnp.bfloat16)
    qkv_cols = [
        jnp.dot(normed, w_qkv[i], preferred_element_type=jnp.float32).astype(jnp.bfloat16) for i in range(3)
    ]
    squares = jnp.stack([jnp.sum(jnp.square(qkv_cols[i].astype(jnp.float32)), axis=-1) for i in range(2)])
    cache_blocks = cache_kv.reshape(2 * frames * own_rows, blocks, wide).transpose(1, 0, 2)
    cached, pieces, squares = exchange(
        1, n, gs, [("block", cache_blocks), ("peer", jnp.stack(qkv_cols)), ("all", squares)]
    )
    inverse = lax.rsqrt(jnp.sum(squares, axis=0) / width + 1e-06)
    pieces = pieces.transpose(1, 2, 0, 3).reshape(3, total_rows, wide)
    gains = lax.dynamic_slice_in_dim(norm_gains, block * wide, wide, axis=1)
    first = place * query_rows
    queries = (
        lax.dynamic_slice_in_dim(pieces[0], first, query_rows, axis=0).astype(jnp.float32)
        * lax.dynamic_slice_in_dim(inverse[0], first, query_rows, axis=0)[:, None]
        * gains[0]
    ).astype(jnp.bfloat16)
    keys_now = (pieces[1].astype(jnp.float32) * inverse[1][:, None] * gains[1]).astype(jnp.bfloat16)
    cached = cached.reshape(n, 2, frames * own_rows, wide).transpose(1, 0, 2, 3).reshape(2, -1, wide)
    keys = jnp.concatenate([cached[0], keys_now], axis=0).reshape(-1, heads, HEAD_DIM)
    values = jnp.concatenate([cached[1], pieces[2]], axis=0).reshape(-1, heads, HEAD_DIM)
    queries = queries.reshape(query_rows, heads, HEAD_DIM)
    scores = jnp.einsum("qhd,khd->hqk", queries, keys, preferred_element_type=jnp.float32) * scale
    expo = jnp.exp(scores - jnp.max(scores, axis=-1, keepdims=True))
    total = jnp.sum(expo, axis=-1, keepdims=True)
    summed = jnp.einsum("hqk,khd->hqd", expo.astype(jnp.bfloat16), values, preferred_element_type=jnp.float32)
    attended = (summed / total).astype(jnp.bfloat16).transpose(1, 0, 2).reshape(query_rows, wide)

    (attended,) = exchange(2, n, gs, [("all", attended)])
    attended = attended.reshape(blocks, total_rows, wide).transpose(1, 0, 2).reshape(total_rows, width)
    projected_cols = jnp.dot(attended, w_out, preferred_element_type=jnp.float32).astype(jnp.bfloat16)
    (projected,) = exchange(3, n, gs, [("all", projected_cols)])
    projected = projected.transpose(1, 0, 2).reshape(total_rows, features)
    residual = all_tokens + modulation[2] * projected.astype(jnp.float32)
    normed2 = (layer_norm(residual) * (1.0 + modulation[4]) + modulation[3]).astype(jnp.bfloat16)
    hidden = jax.nn.gelu(
        jnp.dot(normed2, w_up, preferred_element_type=jnp.float32), approximate=True
    ).astype(jnp.bfloat16)
    partial = jnp.dot(hidden, w_down, preferred_element_type=jnp.float32).astype(jnp.bfloat16)
    feed = reduce_exchange(4, n, partial.reshape(n, own_rows, features))
    own = lax.dynamic_slice_in_dim(residual, me * own_rows, own_rows, axis=0)
    return (own + modulation[5] * feed).astype(jnp.bfloat16)


def solution(mesh):
    n = mesh.shape["seq"]
    in_specs = (
        P(("groups", "seq"), None),
        P(),
        P(None, None, "seq"),
        P(),
        P(None, None, ("groups", "seq"), None),
        P(None, "seq"),
        P(None, "seq"),
        P("seq", None),
    )
    out_specs = P(("groups", "seq"), None)

    def step(*args):
        return local(n, *args)

    return jax.shard_map(step, mesh=mesh, in_specs=in_specs, out_specs=out_specs, check_vma=False)
```
